32 devices in a mesh: seq: 16 (over z, x, core), fsdp: 2 (over y).
Axes of the slice: x: 2, y: 2, z: 4, core: 2. Of those that a mesh axis runs over, the one named last changes fastest.
Arguments:
- block_input: float32 [2, 2048, 1024], P('fsdp', 'seq'), may hold values from -6 to 6
- image_ids: int32 [2, 2048], P('fsdp', 'seq'), may hold values from 0 to 2, as said below
- pad_mask: int32 [2, 2048], P('fsdp', 'seq'), may hold values from 0 to 1, as said below
- cotangent: float32 [2, 2048, 1024], P('fsdp', 'seq'), may hold values from -6 to 6
- w_qkv: float32 [1024, 3072], P(('seq', 'fsdp')), may hold values from -0.21875 to 0.21875
- w_out: float32 [1024, 1024], P(('seq', 'fsdp')), may hold values from -1 to 1
- w_fc1: float32 [1024, 4096], P(('seq', 'fsdp')), may hold values from -0.1875 to 0.1875
- w_fc2: float32 [4096, 1024], P(('seq', 'fsdp')), may hold values from -0.1875 to 0.1875
- ln1_gain: float32 [1024], P(('seq', 'fsdp')), may hold values from 0.25 to 1.75
- ln1_bias: float32 [1024], P(('seq', 'fsdp')), may hold values from -4 to 4
- ln2_gain: float32 [1024], P(('seq', 'fsdp')), may hold values from 0.25 to 1.75
- ln2_bias: float32 [1024], P(('seq', 'fsdp')), may hold values from -4 to 4
- qv_bias: float32 [2048], P(('seq', 'fsdp')), may hold values from -4 to 4
- out_bias: float32 [1024], P(('seq', 'fsdp')), may hold values from -4 to 4
- fc1_bias: float32 [4096], P(('seq', 'fsdp')), may hold values from -6 to 6
- fc2_bias: float32 [1024], P(('seq', 'fsdp')), may hold values from -4 to 4
Outputs:
- block_output: float32 [2, 2048, 1024], P('fsdp', 'seq')
- input_grad: float32 [2, 2048, 1024], P('fsdp', 'seq')
- grad_w_qkv: float32 [1024, 3072], P(('seq', 'fsdp'))
- grad_w_out: float32 [1024, 1024], P(('seq', 'fsdp'))
- grad_w_fc1: float32 [1024, 4096], P(('seq', 'fsdp'))
- grad_w_fc2: float32 [4096, 1024], P(('seq', 'fsdp'))
- grad_ln1_gain: float32 [1024], P(('seq', 'fsdp'))
- grad_ln1_bias: float32 [1024], P(('seq', 'fsdp'))
- grad_ln2_gain: float32 [1024], P(('seq', 'fsdp'))
- grad_ln2_bias: float32 [1024], P(('seq', 'fsdp'))
- grad_qv_bias: float32 [2048], P(('seq', 'fsdp'))
- grad_out_bias: float32 [1024], P(('seq', 'fsdp'))
- grad_fc1_bias: float32 [4096], P(('seq', 'fsdp'))
- grad_fc2_bias: float32 [1024], P(('seq', 'fsdp'))
The draws below stay inside these ranges and needn't reach their ends.
Inputs may be any that keep to these rules, and one draw needn't show every extreme that they name: `image_ids`: each image's 577 tokens are followed by its padding slots, which carry the same id; ids never fall along a stream, every id appears, and in every stream one image has exactly 139 padding slots and none has more. `pad_mask`: 1 on the first 577 slots of each image, 0 on its padding slots.
All inputs are finite; a program needn't handle non-finite values.
Results may differ from the reference program's by a relative error of at most 0.013.
The reference program's roundings to bfloat16 on the way count: a program that leaves them out, or rounds other values in their place, can miss the bound.
Values may be sent and summed in bfloat16 or wider, within the bound.
A program may use at most 256 MiB of HBM per device.

```python
import jax
import jax.numpy as jnp
from jax import lax

D = 1024
HEADS = 16
HD = 64
FF = 4096
IMG_TOK = 577
PAD_SPREAD = 32
STREAMS = 2
STREAM_TOK = 2048
IMGS = 3
PADS = 317
RUN_MOST = 716


def image_layout(key):
    layout_key = jax.random.fold_in(key, 11)
    spread_key, pick_key = jax.random.split(layout_key)
    even_share = PADS // IMGS
    extra_slots = PADS % IMGS
    offsets = jax.random.randint(spread_key, (STREAMS, IMGS), 0, PAD_SPREAD + 1)
    chosen = jax.random.randint(pick_key, (STREAMS, 1), 0, IMGS)
    slot_index = jnp.arange(IMGS)[None, :]
    offsets = jnp.where(slot_index == chosen, PAD_SPREAD, jnp.where(slot_index == (chosen + 1) % IMGS, 0, offsets))
    gap_sizes = even_share + offsets - jnp.roll(offsets, -1, axis=1) + jnp.where(slot_index == chosen, extra_slots, 0)
    run_sizes = IMG_TOK + gap_sizes
    run_ends = jnp.cumsum(run_sizes, axis=1)
    positions = jnp.arange(STREAM_TOK)[None, :, None]
    passed = positions >= run_ends[:, None, :]
    image_index = jnp.sum(passed.astype(jnp.int32), axis=-1)
    run_start = jnp.sum(jnp.where(passed, run_sizes[:, None, :], 0), axis=-1)
    is_token = (positions[:, :, 0] - run_start < IMG_TOK).astype(jnp.int32)
    return (image_index.astype(jnp.int32), is_token)


def draw_image_ids(key, part):
    return image_layout(key)[0]


def draw_pad_mask(key, part):
    return image_layout(key)[1]


def block_scale(stream_key, extent, shards, smallest, top_value):
    def one(position, shards_of):
        draws = jax.random.uniform(jax.random.fold_in(jax.random.fold_in(stream_key, 6), position), (shards_of,), jnp.float32, smallest / len(shards), top_value / len(shards))
        return jnp.repeat(jnp.exp(draws), extent[position] // shards_of).reshape((-1,) + (1,) * (len(extent) - position - 1))

    gain = one(*shards[0])
    for cut in shards[1:]:
        gain = gain * one(*cut)
    return gain


def gaussian(own_key, extent, spread, most, cuts=(), dtype=jnp.bfloat16):
    entries = spread * jax.random.normal(own_key, extent, jnp.float32)
    if cuts:
        entries = entries * block_scale(own_key, extent, cuts, -0.22, 0.18)
    return jnp.clip(entries, -most, most).astype(dtype)


def setup_inputs(seed: int = 0) -> dict:
    key_list = jax.random.split(jax.random.key(seed), 17)
    block_input = gaussian(key_list[0], (STREAMS, STREAM_TOK, D), 1.0, 6.0, ((0, 2), (1, 16)), jnp.float32)
    image_ids = draw_image_ids(jax.random.fold_in(key_list[16], 71), 0)
    pad_mask = draw_pad_mask(jax.random.fold_in(key_list[16], 71), 0)
    cotangent = gaussian(key_list[3], (STREAMS, STREAM_TOK, D), 1.0, 6.0, ((0, 2), (1, 16)), jnp.float32)
    w_qkv = gaussian(key_list[4], (D, 3 * D), (2 * D // 3) ** -0.5, 0.21875, ((0, 32),), jnp.float32)
    w_out = gaussian(key_list[5], (D, D), (D // 32) ** -0.5, 1.0, ((0, 32),), jnp.float32)
    w_fc1 = gaussian(key_list[6], (D, FF), D ** -0.5, 0.1875, ((0, 32),), jnp.float32)
    w_fc2 = gaussian(key_list[7], (FF, D), (FF // 4) ** -0.5, 0.1875, ((0, 32),), jnp.float32)
    ln1_gain = jnp.clip(1.0 + 0.15 * jax.random.normal(key_list[8], (D,), jnp.float32), 0.25, 1.75)
    ln1_bias = gaussian(key_list[9], (D,), 0.3, 4.0, ((0, 32),), jnp.float32)
    ln2_gain = jnp.clip(1.0 + 0.15 * jax.random.normal(key_list[10], (D,), jnp.float32), 0.25, 1.75)
    ln2_bias = gaussian(key_list[11], (D,), 0.3, 4.0, ((0, 32),), jnp.float32)
    qv_bias = gaussian(key_list[12], (2 * D,), 0.3, 4.0, ((0, 32),), jnp.float32)
    out_bias = gaussian(key_list[13], (D,), 0.3, 4.0, ((0, 32),), jnp.float32)
    fc1_bias = gaussian(key_list[14], (FF,), 0.5, 6.0, ((0, 32),), jnp.float32)
    fc2_bias = gaussian(key_list[15], (D,), 0.3, 4.0, ((0, 32),), jnp.float32)
    return dict(block_input=block_input, image_ids=image_ids, pad_mask=pad_mask, cotangent=cotangent, w_qkv=w_qkv, w_out=w_out, w_fc1=w_fc1, w_fc2=w_fc2, ln1_gain=ln1_gain, ln1_bias=ln1_bias, ln2_gain=ln2_gain, ln2_bias=ln2_bias, qv_bias=qv_bias, out_bias=out_bias, fc1_bias=fc1_bias, fc2_bias=fc2_bias)


EPSILON = 1e-05
SCALE = 0.125
NEGATIVE = -1e+30
HIGHEST = lax.Precision.HIGHEST

@jax.custom_vjp
def low(v):
    return lax.optimization_barrier(v.astype(jnp.bfloat16)).astype(jnp.float32)

@jax.custom_vjp
def low_back(v):
    return v

def low_keep(v):
    return (low(v), None)

def low_pass(kept, grad):
    return (grad,)

def back_keep(v):
    return (v, None)

def back_low(kept, grad):
    return (low(grad),)
low.defvjp(low_keep, low_pass)
low_back.defvjp(back_keep, back_low)

def layer_norm(values, norm_gain, norm_shift):
    row_mean = lax.optimization_barrier(jnp.mean(values, axis=-1, keepdims=True))
    centred = values - row_mean
    variance = lax.optimization_barrier(jnp.mean(centred * centred, axis=-1, keepdims=True))
    return centred * lax.rsqrt(variance + EPSILON) * norm_gain + norm_shift

def quick_gelu(values):
    return values * jax.nn.sigmoid(1.702 * values)

def window_forward(slab, weights, key_tag, query_tag, margin, core, sub_rows):
    lowered = tuple((low(item) for item in weights))
    qkv_weight, out_weight, fc1_weight, fc2_weight = (lowered[0], lowered[1], lowered[2], lowered[3])
    gain_one, shift_one, gain_two, shift_two = (lowered[4], lowered[5], lowered[6], lowered[7])
    query_value_bias, attn_bias, hidden_bias, final_bias = (lowered[8], lowered[9], lowered[10], lowered[11])
    normed = low(layer_norm(slab, gain_one, shift_one))
    projected = jnp.dot(normed, qkv_weight, precision=HIGHEST)
    queries = low(low_back(projected[margin:margin + core, :D] + query_value_bias[:D]))
    keys_all = low(low_back(projected[:, D:2 * D]))
    values_all = low(low_back(projected[:, 2 * D:] + query_value_bias[D:]))
    key_span = sub_rows + 2 * margin

    def sub_block(block_index):
        row_start = (block_index * sub_rows).astype(jnp.int32)
        query_heads = lax.dynamic_slice_in_dim(queries, row_start, sub_rows, 0).reshape(sub_rows, HEADS, HD)
        key_heads = lax.dynamic_slice_in_dim(keys_all, row_start, key_span, 0).reshape(key_span, HEADS, HD)
        value_heads = lax.dynamic_slice_in_dim(values_all, row_start, key_span, 0).reshape(key_span, HEADS, HD)
        key_tags = lax.dynamic_slice_in_dim(key_tag, row_start, key_span, 0)
        query_tags = lax.dynamic_slice_in_dim(query_tag, row_start, sub_rows, 0)
        scores = low_back(jnp.einsum('qhd,khd->hqk', query_heads, key_heads, precision=HIGHEST) * SCALE)
        allowed = (query_tags[:, None] == key_tags[None, :]) & (key_tags[None, :] > 0)
        probability = jax.nn.softmax(jnp.where(allowed[None], scores, NEGATIVE), axis=-1)
        mixed_rows = jnp.einsum('hqk,khd->qhd', low(probability), value_heads, precision=HIGHEST)
        return mixed_rows.reshape(sub_rows, D)
    attended = lax.map(jax.checkpoint(sub_block), jnp.arange(core // sub_rows).astype(jnp.int32))
    attended = low(low_back(attended.reshape(core, D)))
    residual = slab[margin:margin + core]
    mid_stream = residual + low_back(jnp.dot(attended, out_weight, precision=HIGHEST) + attn_bias)
    normed_two = low(layer_norm(mid_stream, gain_two, shift_two))
    pre_act = low_back(jnp.dot(normed_two, fc1_weight, precision=HIGHEST) + hidden_bias)
    hidden = low(quick_gelu(pre_act))
    return mid_stream + low_back(jnp.dot(hidden, fc2_weight, precision=HIGHEST) + final_bias)

def reference(block_input, image_ids, pad_mask, cotangent, w_qkv, w_out, w_fc1, w_fc2, ln1_gain, ln1_bias, ln2_gain, ln2_bias, qv_bias, out_bias, fc1_bias, fc2_bias):
    weights = (w_qkv, w_out, w_fc1, w_fc2, ln1_gain, ln1_bias, ln2_gain, ln2_bias, qv_bias, out_bias, fc1_bias, fc2_bias)
    margin = RUN_MOST
    sub_rows = 512
    group = max(1, min(IMGS, 4096 // RUN_MOST))
    block_count = (IMGS + group - 1) // group
    core = (group * RUN_MOST + sub_rows - 1) // sub_rows * sub_rows
    window = core + 2 * margin
    padded_len = STREAM_TOK + window
    row_pad = ((0, 0), (margin, core + margin), (0, 0))
    tag_pad = ((0, 0), (margin, core + margin))
    input_pad = jnp.pad(block_input, row_pad)
    cot_pad = jnp.pad(cotangent, row_pad)
    id_pad = jnp.pad(image_ids, tag_pad, constant_values=-1)
    mask_pad = jnp.pad(pad_mask, tag_pad, constant_values=0)
    key_tags = jnp.where(mask_pad == 1, id_pad + 1, 0).astype(jnp.int32)
    query_tags = (id_pad + 1).astype(jnp.int32)
    zero_index = jnp.zeros((), jnp.int32)

    def step(carry, pair):
        out_acc, grad_acc, grad_sum = carry
        stream = (pair // block_count).astype(jnp.int32)
        block_index = (pair % block_count).astype(jnp.int32)
        first = (block_index * group).astype(jnp.int32)
        stream_ids = lax.dynamic_index_in_dim(image_ids, stream, 0, keepdims=False)
        row_start = jnp.sum((stream_ids < first).astype(jnp.int32)).astype(jnp.int32)
        core_start = (row_start + margin).astype(jnp.int32)
        slab = lax.dynamic_slice(input_pad, (stream, row_start, zero_index), (1, window, D))[0]
        slab_keys = lax.dynamic_slice(key_tags, (stream, row_start), (1, window))[0]
        slab_queries = lax.dynamic_slice(query_tags, (stream, core_start), (1, core))[0]
        core_ids = lax.dynamic_slice(id_pad, (stream, core_start), (1, core))[0]
        member = (core_ids >= first) & (core_ids < first + group)
        core_cot = lax.dynamic_slice(cot_pad, (stream, core_start, zero_index), (1, core, D))[0]
        core_cot = jnp.where(member[:, None], core_cot, 0.0)
        result, pullback = jax.vjp(lambda slab_in, weight_in: window_forward(slab_in, weight_in, slab_keys, slab_queries, margin, core, sub_rows), slab, weights)
        grad_slab, grad_weights = pullback(core_cot)
        out_old = lax.dynamic_slice(out_acc, (stream, core_start, zero_index), (1, core, D))
        out_new = out_old + jnp.where(member[:, None], result, 0.0)[None]
        out_acc = lax.dynamic_update_slice(out_acc, out_new, (stream, core_start, zero_index))
        grad_old = lax.dynamic_slice(grad_acc, (stream, core_start, zero_index), (1, core, D))
        grad_new = grad_old + jnp.where(member[:, None], grad_slab[margin:margin + core], 0.0)[None]
        grad_acc = lax.dynamic_update_slice(grad_acc, grad_new, (stream, core_start, zero_index))
        grad_sum = jax.tree.map(jnp.add, grad_sum, grad_weights)
        return ((out_acc, grad_acc, grad_sum), None)
    start_carry = (jnp.zeros((STREAMS, padded_len, D), jnp.float32), jnp.zeros((STREAMS, padded_len, D), jnp.float32), tuple((jnp.zeros_like(item) for item in weights)))
    pairs = jnp.arange(STREAMS * block_count).astype(jnp.int32)
    final_carry, _ = lax.scan(step, start_carry, pairs)
    out_acc, grad_acc, grad_sum = final_carry
    block_output = out_acc[:, margin:margin + STREAM_TOK]
    input_grad = grad_acc[:, margin:margin + STREAM_TOK]
    return (block_output, input_grad, grad_sum[0], grad_sum[1], grad_sum[2], grad_sum[3], grad_sum[4], grad_sum[5], grad_sum[6], grad_sum[7], grad_sum[8], grad_sum[9], grad_sum[10], grad_sum[11])
```

```python
import jax
import jax.numpy as jnp
from jax import lax
from jax.sharding import PartitionSpec as P

HEADS = 16
IMG_TOK = 577
PAD_SPREAD = 32


EPSILON = 1e-05
SCALE = 0.125
NEGATIVE = -1e30


def shifted(block, axis, distance):
    devices = range(lax.axis_size(axis))
    route = [(i - distance, i) for i in devices if i - distance in devices]
    return lax.ppermute(block, axis, route)


def layer_norm(values, norm_gain, norm_shift):
    row_mean = jnp.mean(values, axis=-1, keepdims=True)
    centred = values - row_mean
    variance = jnp.mean(centred * centred, axis=-1, keepdims=True)
    return centred * lax.rsqrt(variance + EPSILON) * norm_gain + norm_shift


def quick_gelu(values):
    return values * jax.nn.sigmoid(1.702 * values)


def allowed_pairs(query_tag, key_tag):
    key_float = key_tag.astype(jnp.float32)
    return (query_tag[:, None] == key_float[None, :]) & (key_float[None, :] > 0.0)


def head_scores(query_heads, key_block, head_count):
    key_heads = key_block.reshape(key_block.shape[0], head_count, -1)
    return (
        jnp.einsum("qhd,khd->hqk", query_heads, key_heads, preferred_element_type=jnp.float32)
        * SCALE
    )


def pair_grads(
    query_heads,
    grad_heads,
    log_total,
    delta_rows,
    query_tag,
    key_block,
    value_block,
    key_tag,
    head_count,
):
    key_heads = key_block.reshape(key_block.shape[0], head_count, -1)
    value_heads = value_block.reshape(value_block.shape[0], head_count, -1)
    scores = (
        jnp.einsum("qhd,khd->hqk", query_heads, key_heads, preferred_element_type=jnp.float32)
        * SCALE
    )
    allowed = allowed_pairs(query_tag, key_tag)[None]
    probability = jnp.where(allowed, jnp.exp(scores - log_total[:, :, None]), 0.0)
    grad_prob = jnp.einsum(
        "qhd,khd->hqk", grad_heads, value_heads, preferred_element_type=jnp.float32
    )
    grad_scores = (probability * (grad_prob - delta_rows[:, :, None])).astype(jnp.bfloat16)
    grad_query = (
        jnp.einsum("hqk,khd->qhd", grad_scores, key_heads, preferred_element_type=jnp.float32)
        * SCALE
    )
    grad_key = (
        jnp.einsum("hqk,qhd->khd", grad_scores, query_heads, preferred_element_type=jnp.float32)
        * SCALE
    )
    grad_value = jnp.einsum(
        "hqk,qhd->khd",
        probability.astype(jnp.bfloat16),
        grad_heads,
        preferred_element_type=jnp.float32,
    )
    query_rows = query_heads.shape[0]
    key_rows = key_heads.shape[0]
    return (
        grad_query.reshape(query_rows, -1),
        grad_key.reshape(key_rows, -1),
        grad_value.reshape(key_rows, -1),
    )


def gather_weight(shard):
    return lax.all_gather(shard.astype(jnp.bfloat16), ("seq", "fsdp"), axis=0, tiled=True)


def gather_small(shards):
    parts = lax.axis_size(("seq", "fsdp"))
    packed = jnp.concatenate([item.astype(jnp.bfloat16) for item in shards])
    whole = lax.all_gather(packed, ("seq", "fsdp"), axis=0, tiled=False)
    outs = []
    offset = 0
    for item in shards:
        width = item.shape[0]
        outs.append(whole[:, offset : offset + width].reshape(parts * width).astype(jnp.float32))
        offset += width
    return tuple(outs)


def scatter_weight(term):
    low_term = term.astype(jnp.bfloat16)
    return lax.psum_scatter(low_term, ("seq", "fsdp"), scatter_dimension=0, tiled=True).astype(
        jnp.float32
    )


def scatter_small(terms):
    parts = lax.axis_size(("seq", "fsdp"))
    packed = jnp.concatenate([item.reshape(parts, -1) for item in terms], axis=1)
    mine = lax.psum_scatter(packed, ("seq", "fsdp"), scatter_dimension=0, tiled=True).reshape(-1)
    outs = []
    offset = 0
    for item in terms:
        width = item.shape[0] // parts
        outs.append(mine[offset : offset + width])
        offset += width
    return tuple(outs)


def local(
    block_input,
    image_ids,
    pad_mask,
    cotangent,
    w_qkv,
    w_out,
    w_fc1,
    w_fc2,
    ln1_gain,
    ln1_bias,
    ln2_gain,
    ln2_bias,
    qv_bias,
    out_bias,
    fc1_bias,
    fc2_bias,
):
    row_count = block_input.shape[1]
    model_width = block_input.shape[2]
    head_count = HEADS
    head_size = model_width // head_count
    seq_devices = lax.axis_size("seq")
    stream_len = row_count * seq_devices
    image_count = stream_len // (IMG_TOK + IMG_TOK // 8)
    pad_total = stream_len - image_count * IMG_TOK
    gap_most = pad_total // image_count + pad_total % image_count + PAD_SPREAD
    neighbour_reach = (IMG_TOK + gap_most + row_count - 2) // row_count
    distances = []
    for step_size in range(1, neighbour_reach + 1):
        distances = distances + [step_size, -step_size]
    inputs = block_input.reshape(row_count, model_width)
    grad_output = cotangent.reshape(row_count, model_width)
    own_ids = image_ids.reshape(row_count)
    own_mask = pad_mask.reshape(row_count)
    query_tag = (own_ids + 1).astype(jnp.float32)
    key_tag = jnp.where(own_mask == 1, own_ids + 1, 0).astype(jnp.bfloat16)
    small_params = (ln1_gain, ln1_bias, ln2_gain, ln2_bias, qv_bias, out_bias, fc1_bias, fc2_bias)
    small_gathered = gather_small(small_params)
    qkv_weight = gather_weight(w_qkv)
    out_weight = gather_weight(w_out)
    fc1_weight = gather_weight(w_fc1)
    fc2_weight = gather_weight(w_fc2)
    gain_one, shift_one, gain_two, shift_two = small_gathered[:4]
    query_value_bias, attn_bias, hidden_bias, final_bias = small_gathered[4:]
    normed = layer_norm(inputs, gain_one, shift_one).astype(jnp.bfloat16)
    projected = jnp.dot(normed, qkv_weight, preferred_element_type=jnp.float32)
    query = (projected[:, :model_width] + query_value_bias[:model_width]).astype(jnp.bfloat16)
    keys = projected[:, model_width : 2 * model_width].astype(jnp.bfloat16)
    values = (projected[:, 2 * model_width :] + query_value_bias[model_width:]).astype(jnp.bfloat16)
    query_heads = query.reshape(row_count, head_count, head_size)
    received = []
    for distance in distances:
        received = received + [shifted((keys, values, key_tag), "seq", distance)]
    pieces = [(keys, values, key_tag)] + received
    row_top = jnp.full((head_count, row_count), NEGATIVE, jnp.float32)
    row_total = jnp.zeros((head_count, row_count), jnp.float32)
    for neighbour in pieces:
        scores = head_scores(query_heads, neighbour[0], head_count)
        allowed = allowed_pairs(query_tag, neighbour[2])[None]
        new_top = jnp.maximum(row_top, jnp.max(jnp.where(allowed, scores, NEGATIVE), axis=-1))
        fresh = jnp.sum(jnp.where(allowed, jnp.exp(scores - new_top[:, :, None]), 0.0), axis=-1)
        row_total = row_total * jnp.exp(row_top - new_top) + fresh
        row_top = new_top
    log_total = row_top + jnp.log(row_total)
    attn_sum = jnp.zeros((row_count, head_count, head_size), jnp.float32)
    for neighbour in pieces:
        scores = head_scores(query_heads, neighbour[0], head_count)
        allowed = allowed_pairs(query_tag, neighbour[2])[None]
        probs_low = jnp.where(allowed, jnp.exp(scores - log_total[:, :, None]), 0.0).astype(
            jnp.bfloat16
        )
        value_heads = neighbour[1].reshape(-1, head_count, head_size)
        attn_sum = attn_sum + jnp.einsum(
            "hqk,khd->qhd", probs_low, value_heads, preferred_element_type=jnp.float32
        )
    attn_full = attn_sum.reshape(row_count, model_width)
    attn_low = attn_full.astype(jnp.bfloat16)
    mid_stream = (
        inputs + jnp.dot(attn_low, out_weight, preferred_element_type=jnp.float32) + attn_bias
    )
    normed_two = layer_norm(mid_stream, gain_two, shift_two).astype(jnp.bfloat16)
    pre_act = jnp.dot(normed_two, fc1_weight, preferred_element_type=jnp.float32) + hidden_bias
    hidden = quick_gelu(pre_act).astype(jnp.bfloat16)
    block_output = (
        mid_stream + jnp.dot(hidden, fc2_weight, preferred_element_type=jnp.float32) + final_bias
    )
    back_qkv, back_out, back_fc1, back_fc2 = (qkv_weight, out_weight, fc1_weight, fc2_weight)
    back_gain_one = gain_one
    back_gain_two = gain_two
    grad_low = grad_output.astype(jnp.bfloat16)
    grad_fc2_weight = jnp.einsum("tf,td->fd", hidden, grad_low, preferred_element_type=jnp.float32)
    grad_final_bias = jnp.sum(grad_low.astype(jnp.float32), axis=0)
    grad_hidden = jnp.einsum("td,fd->tf", grad_low, back_fc2, preferred_element_type=jnp.float32)
    _, gelu_back = jax.vjp(quick_gelu, pre_act)
    grad_pre = gelu_back(grad_hidden)[0].astype(jnp.bfloat16)
    grad_fc1_weight = jnp.einsum(
        "td,tf->df", normed_two, grad_pre, preferred_element_type=jnp.float32
    )
    grad_hidden_bias = jnp.sum(grad_pre.astype(jnp.float32), axis=0)
    grad_normed_two = jnp.einsum(
        "tf,df->td", grad_pre, back_fc1, preferred_element_type=jnp.float32
    )
    _, norm_two_back = jax.vjp(layer_norm, mid_stream, back_gain_two, shift_two)
    grad_mid_norm, grad_gain_two, grad_shift_two = norm_two_back(grad_normed_two)
    grad_mid = grad_output + grad_mid_norm
    grad_mid_low = grad_mid.astype(jnp.bfloat16)
    grad_out_weight = jnp.einsum(
        "td,te->de", attn_low, grad_mid_low, preferred_element_type=jnp.float32
    )
    grad_attn_bias = jnp.sum(grad_mid_low.astype(jnp.float32), axis=0)
    grad_attn = jnp.einsum(
        "te,de->td", grad_mid_low, back_out, preferred_element_type=jnp.float32
    ).astype(jnp.bfloat16)
    delta_rows = jnp.sum(
        (grad_attn.astype(jnp.float32) * attn_full).reshape(row_count, head_count, head_size),
        axis=-1,
    ).T
    grad_heads = grad_attn.reshape(row_count, head_count, head_size)
    grad_query, grad_key, grad_value = pair_grads(
        query_heads, grad_heads, log_total, delta_rows, query_tag, keys, values, key_tag, head_count
    )
    for distance, neighbour in zip(distances, received):
        part_query, part_key, part_value = pair_grads(
            query_heads,
            grad_heads,
            log_total,
            delta_rows,
            query_tag,
            neighbour[0],
            neighbour[1],
            neighbour[2],
            head_count,
        )
        grad_query = grad_query + part_query
        returned = (
            shifted(part_key.astype(jnp.bfloat16), "seq", -distance).astype(part_key.dtype),
            shifted(part_value.astype(jnp.bfloat16), "seq", -distance).astype(part_value.dtype),
        )
        grad_key = grad_key + returned[0]
        grad_value = grad_value + returned[1]
    grad_query_low = grad_query.astype(jnp.bfloat16)
    grad_key_low = grad_key.astype(jnp.bfloat16)
    grad_value_low = grad_value.astype(jnp.bfloat16)
    grad_qkv = jnp.concatenate([grad_query_low, grad_key_low, grad_value_low], axis=1)
    grad_qkv_weight = jnp.einsum("td,te->de", normed, grad_qkv, preferred_element_type=jnp.float32)
    grad_query_value_bias = jnp.concatenate(
        [
            jnp.sum(grad_query_low.astype(jnp.float32), axis=0),
            jnp.sum(grad_value_low.astype(jnp.float32), axis=0),
        ]
    )
    grad_normed = jnp.einsum("te,de->td", grad_qkv, back_qkv, preferred_element_type=jnp.float32)
    _, norm_one_back = jax.vjp(layer_norm, inputs, back_gain_one, shift_one)
    grad_input_norm, grad_gain_one, grad_shift_one = norm_one_back(grad_normed)
    input_grad = grad_mid + grad_input_norm
    terms = [
        grad_qkv_weight,
        grad_out_weight,
        grad_fc1_weight,
        grad_fc2_weight,
        grad_gain_one,
        grad_shift_one,
        grad_gain_two,
        grad_shift_two,
        grad_query_value_bias,
        grad_attn_bias,
        grad_hidden_bias,
        grad_final_bias,
    ]
    reduced = tuple(scatter_weight(term) for term in terms[:4]) + scatter_small(terms[4:])
    return (
        block_output.reshape(block_input.shape),
        input_grad.reshape(block_input.shape),
        reduced[0],
        reduced[1],
        reduced[2],
        reduced[3],
        reduced[4],
        reduced[5],
        reduced[6],
        reduced[7],
        reduced[8],
        reduced[9],
        reduced[10],
        reduced[11],
    )


def solution(mesh):
    return jax.shard_map(
        local,
        mesh=mesh,
        in_specs=(
            P("fsdp", "seq", None),
            P("fsdp", "seq"),
            P("fsdp", "seq"),
            P("fsdp", "seq", None),
            P(("seq", "fsdp"), None),
            P(("seq", "fsdp"), None),
            P(("seq", "fsdp"), None),
            P(("seq", "fsdp"), None),
            P(("seq", "fsdp")),
            P(("seq", "fsdp")),
            P(("seq", "fsdp")),
            P(("seq", "fsdp")),
            P(("seq", "fsdp")),
            P(("seq", "fsdp")),
            P(("seq", "fsdp")),
            P(("seq", "fsdp")),
        ),
        out_specs=(
            P("fsdp", "seq", None),
            P("fsdp", "seq", None),
            P(("seq", "fsdp"), None),
            P(("seq", "fsdp"), None),
            P(("seq", "fsdp"), None),
            P(("seq", "fsdp"), None),
            P(("seq", "fsdp")),
            P(("seq", "fsdp")),
            P(("seq", "fsdp")),
            P(("seq", "fsdp")),
            P(("seq", "fsdp")),
            P(("seq", "fsdp")),
            P(("seq", "fsdp")),
            P(("seq", "fsdp")),
        ),
        check_vma=False,
    )
```
